256 devices in a mesh: dp: 64 (over x, z_lo, y), pipe: 4 (over z_hi, core).
Axes of the slice: x: 4, y: 4, z: 8 (z_hi: 2, z_lo: 4; z = z_hi * 4 + z_lo), core: 2. Of those that a mesh axis runs over, the one named last changes fastest.
Arguments:
- hidden: bfloat16 [16384, 2048], P('dp'), may hold values from -16 to 16
- gain: float32 [2048], replicated, may hold values from 0.25 to 1.75
- w_value: bfloat16 [4, 2048, 2048], P('pipe', 'dp'), may hold values from -0.125 to 0.125
- d_value: bfloat16 [4, 16384, 2048], P('pipe', 'dp'), may hold values from -3 to 3
Outputs:
- grad_hidden: bfloat16 [16384, 2048], P('dp')
- grad_gain: float32 [2048], P('dp')
- grad_value: float32 [4, 2048, 2048], P('pipe', 'dp')
The draws below stay inside these ranges and needn't reach their ends.
All inputs are finite; a program needn't handle non-finite values.
Results may differ from the reference program's by a relative error of at most 0.0029.
Values may be sent and summed in bfloat16 or wider, within the bound.
No kernel may reach another device: no remote copies, remote signals or barrier semaphores. Data moves between devices by JAX's collectives and lax.ppermute only.
A program may use at most 64 MiB of HBM per device.

```python
import jax
import jax.numpy as jnp
from jax import lax

D = 2048
KV = 2048
TOKENS = 16384
SECTIONS = 4
N_DP = 64


def raised(values, rng, source, target, parts, factor):
    owner, partner = [(jnp.arange(values.shape[axis_at]) // (values.shape[axis_at] // parts)).reshape([-1 if axis == axis_at else 1 for axis in range(values.ndim)]) for axis_at in (source, target)]
    chosen = jax.random.permutation(rng, parts)[partner]
    strong = (owner == chosen) | (owner == (partner + parts // 2) % parts)
    return jnp.where(strong, factor * values, values)


def steps_of(own_key, dims, shards, least, top_value):
    def one(axis_at, blocks):
        steps = jax.random.uniform(jax.random.fold_in(jax.random.fold_in(own_key, 6), axis_at), (blocks,), jnp.float32, least / len(shards), top_value / len(shards))
        return jnp.repeat(jnp.exp(steps), dims[axis_at] // blocks).reshape((-1,) + (1,) * (len(dims) - axis_at - 1))

    level = one(*shards[0])
    for cut in shards[1:]:
        level = level * one(*cut)
    return level


def noise(own_key, shape, width, bound, pieces=(), kind=jnp.bfloat16):
    array = jax.random.normal(own_key, shape, jnp.float32) * width
    if len(pieces) > 0:
        array = steps_of(own_key, shape, pieces, -0.22, 0.18) * array
    return jnp.clip(array, min=-bound, max=bound).astype(kind)


def bell_draw_with(rng, dims, scale, reach, shards, heavy, held_as=jnp.bfloat16):
    result = scale * jax.random.normal(rng, dims, jnp.float32)
    if shards:
        result = result * steps_of(rng, dims, shards, -0.22, 0.18)
    return jnp.clip(raised(result, jax.random.fold_in(rng, 3), *heavy), -reach, reach).astype(held_as)


def setup_inputs(seed: int = 0) -> dict:
    keys = jax.random.split(jax.random.key(seed), 5)
    return {
        "hidden": bell_draw_with(keys[0], (TOKENS, D), 1.0, 16.0, ((0, 64),), (0, 1, 64, 4.0)),
        "gain": jnp.clip(1.0 + 0.15 * jax.random.normal(keys[1], (D,), jnp.float32), 0.25, 1.75),
        "w_value": noise(keys[2], (SECTIONS, D, KV), D ** -0.5, 0.125, ((0, 4), (1, 64))),
        "d_value": noise(keys[3], (SECTIONS, TOKENS, KV), 0.5, 3.0, ((0, 4), (1, 64))),
    }


epsilon = 1e-06

def reference(hidden, gain, w_value, d_value):
    hidden_f = hidden.astype(jnp.float32)
    row_scale = jnp.sqrt(lax.optimization_barrier(jnp.mean(hidden_f * hidden_f, axis=-1, keepdims=True)) + epsilon)
    normed = hidden_f / row_scale
    encoded = (normed * gain).astype(jnp.bfloat16)
    grad_encoded = jnp.zeros(hidden.shape, jnp.float32)
    value_list = []
    for section in range(SECTIONS):
        grad_encoded = grad_encoded + lax.dot_general(d_value[section], w_value[section], (((1,), (1,)), ((), ())), preferred_element_type=jnp.float32)
        value_list.append(lax.dot_general(encoded, d_value[section], (((0,), (0,)), ((), ())), preferred_element_type=jnp.float32) / N_DP)
    grad_gain = lax.optimization_barrier(jnp.sum(grad_encoded * normed, axis=0)) / N_DP
    scaled = gain * grad_encoded
    grad_hidden = ((scaled - normed * lax.optimization_barrier(jnp.mean(scaled * normed, axis=-1, keepdims=True))) / row_scale).astype(jnp.bfloat16)
    return (grad_hidden, grad_gain, jnp.stack(value_list))
```

```python
import jax
import jax.numpy as jnp
from jax import lax
from jax.sharding import PartitionSpec as P

epsilon = 1e-06
F32, BF16 = jnp.float32, jnp.bfloat16
AXES = ("dp", "pipe")


def pairs(dx=0, dy=0, dl=0, dh=0, dc=0):
    out = []
    for x in range(4):
        for zl in range(4):
            for y in range(4):
                for zh in range(2):
                    for c in range(2):
                        source = (((x * 4 + zl) * 4 + y) * 2 + zh) * 2 + c
                        target = ((((x + dx) % 4 * 4 + (zl + dl) % 4) * 4 + (y + dy) % 4) * 2 + (zh + dh) % 2) * 2 + (c + dc) % 2
                        out.append((source, target))
    return out


def send(value, **shift):
    return lax.ppermute(value, AXES, pairs(**shift))


def pick(stack, index):
    return lax.dynamic_index_in_dim(stack, index, 0, keepdims=False)


def mm(a, b, dims):
    return lax.dot_general(a, b, (dims, ((), ())), preferred_element_type=F32)


def local(hidden, gain, w_value, d_value):
    dp, pipe = lax.axis_index("dp"), lax.axis_index("pipe")
    x, zl, y = dp // 16, dp // 4 % 4, dp % 4
    zh, c = pipe // 2, pipe % 2
    d, w = d_value[0], w_value[0]

    hidden_f = hidden.astype(F32)
    row_scale = jnp.sqrt(jnp.mean(hidden_f * hidden_f, axis=-1, keepdims=True) + epsilon)
    normed = hidden_f / row_scale
    encoded = (normed * gain).astype(BF16)

    def piece(q):
        return lax.dynamic_slice(encoded, (c * 128, q % 4 * 512), (128, 512))

    e_l = send(piece(x + 1), dx=1)
    e_r = send(piece(x + 3), dx=3)
    e_f = send(piece(x + 2), dx=2)
    mine = jnp.stack([e_l, e_f, e_r])
    other = send(mine, dc=1)
    e_blocks = jnp.where(c == 0, jnp.concatenate([mine, other], 1), jnp.concatenate([other, mine], 1))
    e_own = lax.dynamic_slice(encoded, (0, x * 512), (256, 512))
    e_all = jnp.concatenate([e_own[None], e_blocks]).reshape(1024, 512)

    halves = []
    for h in range(2):
        part = d[:, h * 1024 : (h + 1) * 1024]
        left = send(part, dx=1)
        right = send(part, dx=3)
        far_a = send(left[:128], dx=1)
        far_b = send(right[128:], dx=3)
        halves.append((part, left, jnp.concatenate([far_a, far_b]), right))

    z_stack = jnp.stack([w] + [send(w, dl=k) for k in (1, 2, 3)])
    z_rows = z_stack.reshape(128, 2048)
    w_l = send(z_rows, dy=1)
    w_r = send(z_rows, dy=3)
    w_fa = send(w_l[:64], dy=1)
    w_fb = send(w_r[64:], dy=3)
    y_stack = jnp.stack([z_rows, w_l, jnp.concatenate([w_fa, w_fb]), w_r]).reshape(4, 4, 32, 2048)
    rows = []
    for jz in range(4):
        for jy in range(4):
            rows.append(lax.dynamic_slice(y_stack, ((y - jy) % 4, (zl - jz) % 4, 0, 0), (1, 1, 32, 2048)).reshape(32, 2048))
    w_rows = jnp.concatenate(rows)

    terms = []
    for k in range(4):
        terms.append(
            mm(halves[0][k], w_rows[:, :1024], ((1,), (1,))) + mm(halves[1][k], w_rows[:, 1024:], ((1,), (1,)))
        )
    p = jnp.stack(terms)

    def half_of(v, at):
        return lax.dynamic_slice(v, (0, at * 128, 0), (v.shape[0], 128, 512))

    s = half_of(p, c) + send(half_of(p, 1 - c), dc=1)

    def quarter(v, at):
        return lax.dynamic_slice(v, (at * 64, 0), (64, 512))

    pieces = []
    for k, shift in ((0, 0), (1, 3), (2, 2), (3, 1)):
        own = quarter(s[k], zh)
        if shift:
            own = send(own, dx=shift)
        pieces.append(own + send(quarter(s[k], 1 - zh).astype(BF16), dx=shift, dh=1).astype(F32))
    piece_stack = jnp.stack(pieces)
    grad = jnp.concatenate([pick(piece_stack, (q - x) % 4) for q in range(4)], axis=1)

    at = c * 128 + zh * 64
    normed_q = lax.dynamic_slice(normed, (at, 0), (64, 2048))
    scale_q = lax.dynamic_slice(row_scale, (at, 0), (64, 1))
    scaled = gain * grad
    result = ((scaled - normed_q * jnp.mean(scaled * normed_q, axis=-1, keepdims=True)) / scale_q).astype(BF16)
    across = send(result, dh=1)
    own_core = jnp.where(zh == 0, jnp.stack([result, across]), jnp.stack([across, result]))
    other_core = send(own_core, dc=1)
    grad_hidden = jnp.where(c == 0, jnp.stack([own_core, other_core]), jnp.stack([other_core, own_core])).reshape(256, 2048)

    outs = []
    gain_terms = [0.0] * 4
    for h in range(2):
        part = mm(e_all, jnp.concatenate(halves[h]), ((0,), (0,))).reshape(4, 4, 32, 1024)

        def to_y(k, part=part):
            return lax.dynamic_index_in_dim(part, (y + k) % 4, 1, keepdims=False)

        total = to_y(0)
        for k in (1, 2, 3):
            total = total + send(to_y(k).astype(BF16), dy=k).astype(F32)
        mine = pick(total, zl)
        for k in range(4):
            block = pick(total, (zl + k) % 4)
            w_block = z_stack[(4 - k) % 4][:, h * 1024 : (h + 1) * 1024].astype(F32)
            gain_terms[k] = gain_terms[k] + jnp.sum(block * w_block, axis=1)
            if k:
                mine = mine + send(block.astype(BF16), dl=k).astype(F32)
        outs.append(mine / 64)
    grad_value = jnp.concatenate(outs, axis=1)

    g = gain_terms[0]
    for k in (1, 2, 3):
        g = g + send(gain_terms[k], dl=k)
    g = g + send(g, dc=1)
    g = g + send(g, dh=1)
    grad_gain = g / (64 * lax.dynamic_slice(gain, (dp * 32,), (32,)))
    return (grad_hidden, grad_gain, grad_value[None])


def solution(mesh):
    return jax.shard_map(
        local,
        mesh=mesh,
        in_specs=(P("dp", None), P(), P("pipe", "dp", None), P("pipe", "dp", None)),
        out_specs=(P("dp", None), P("dp"), P("pipe", "dp", None)),
        check_vma=False,
    )
```

```python
import jax
import jax.numpy as jnp
from jax import lax
from jax.experimental import pallas as pl
from jax.experimental.pallas import tpu as pltpu
from jax.sharding import PartitionSpec as P

epsilon = 1e-06
F32, BF16 = jnp.float32, jnp.bfloat16
AXES = ("dp", "pipe")
VMEM = pl.BlockSpec(memory_space=pltpu.VMEM)
SMEM = pl.BlockSpec(memory_space=pltpu.SMEM)


def pairs(dx=0, dy=0, dl=0, dh=0, dc=0):
    out = []
    for x in range(4):
        for zl in range(4):
            for y in range(4):
                for zh in range(2):
                    for c in range(2):
                        source = (((x * 4 + zl) * 4 + y) * 2 + zh) * 2 + c
                        target = ((((x + dx) % 4 * 4 + (zl + dl) % 4) * 4 + (y + dy) % 4) * 2 + (zh + dh) % 2) * 2 + (c + dc) % 2
                        out.append((source, target))
    return out


def send(value, **shift):
    return lax.ppermute(value, AXES, pairs(**shift))


def call(body, outs, flops, *args, scratch=()):
    shapes = [jax.ShapeDtypeStruct(s, t) for s, t in outs]
    moved = sum(v.size * v.dtype.itemsize for v in args) + sum(v.size * v.dtype.itemsize for v in shapes)
    return pl.pallas_call(
        body,
        out_shape=shapes,
        in_specs=[SMEM] + [VMEM] * (len(args) - 1),
        out_specs=[VMEM] * len(shapes),
        scratch_shapes=list(scratch),
        cost_estimate=pl.CostEstimate(flops=flops, bytes_accessed=moved, transcendentals=0),
        compiler_params=pltpu.CompilerParams(vmem_limit_bytes=40 * 1024 * 1024),
    )(*args)


def at(start, size, multiple):
    return pl.ds(pl.multiple_of(start, multiple), size)


def norm_kernel(idx, h, gain, own, p1, p2, p3, scale):
    x, c = idx[0], idx[4]
    h_all = h[...].astype(F32)
    scale[...] = jnp.broadcast_to(jnp.sqrt(jnp.mean(h_all * h_all, axis=-1, keepdims=True) + epsilon), (256, 128))
    columns = at(x * 512, 512, 512)
    own[...] = (h[:, columns].astype(F32) / scale[:, :1] * gain[:, columns]).astype(BF16)
    rows = at(c * 128, 128, 128)
    for k, out in ((1, p1), (2, p2), (3, p3)):
        columns = at((x + k) % 4 * 512, 512, 512)
        out[...] = (h[rows, columns].astype(F32) / scale[rows, :1] * gain[:, columns]).astype(BF16)


def value_kernel(idx, e_own, m1, m2, m3, oth, d0, d1, l0, l1, fa, fb, r0, r1, own, s1, s2, s3, tmp):
    y, c = idx[1], idx[4]

    def dot(a, b):
        return lax.dot_general(a, b, (((0,), (0,)), ((), ())), preferred_element_type=F32)

    def column(j, carry):
        columns = at(j * 256, 256, 256)
        acc = dot(e_own[:128], d0[:, columns]) + dot(e_own[128:], d1[:, columns])
        for k, lo, hi, mine in ((0, l0, l1, m1), (1, fa, fb, m2), (2, r0, r1, m3)):
            first = jnp.where(c == 0, lo[:, columns], hi[:, columns])
            second = jnp.where(c == 0, hi[:, columns], lo[:, columns])
            acc = acc + dot(mine[...], first) + dot(oth[k], second)
        tmp[...] = acc
        for zl in range(4):
            rows = pl.ds(zl * 32, 32)
            own[rows, columns] = tmp[at(zl * 128 + y * 32, 32, 32), :]
            for k, out in ((1, s1), (2, s2), (3, s3)):
                out[rows, columns] = tmp[at(zl * 128 + (y + k) % 4 * 32, 32, 32), :].astype(BF16)
        return carry

    lax.fori_loop(0, 8, column, 0)


def encoded_grad_kernel(idx, w0, w1, w2, w3, d0, d1, l0, l1, fa, fb, r0, r1, keep, give, w):
    y, zl, c = idx[1], idx[2], idx[4]
    for k, block in enumerate((w0, w1, w2, w3)):
        jy = (y + 4 - k) % 4
        for r in range(4):
            jz = (zl + 4 - r) % 4
            w[at((jz * 4 + jy) * 32, 32, 32), :] = block[r * 32 : (r + 1) * 32, :]

    def column(j, carry):
        rows = at(j * 256, 256, 256)
        columns = at(j * 256, 256, 256)
        part = w[rows, :]
        for k, (lo, hi) in enumerate(((d0, d1), (l0, l1), (fa, fb), (r0, r1))):
            p_lo = lax.dot_general(lo[...], part, (((1,), (1,)), ((), ())), preferred_element_type=F32)
            p_hi = lax.dot_general(hi[...], part, (((1,), (1,)), ((), ())), preferred_element_type=F32)
            keep[k, :, columns] = jnp.where(c == 0, p_lo, p_hi)
            give[k, :, columns] = jnp.where(c == 0, p_hi, p_lo)
        return carry

    lax.fori_loop(0, 2, column, 0)


def core_sum_kernel(idx, keep, got, own, give):
    zh = idx[3]
    mine, theirs = at(zh * 64, 64, 64), at((1 - zh) * 64, 64, 64)
    for k in range(4):
        own[k] = keep[k, mine, :] + got[k, mine, :]
        give[k] = (keep[k, theirs, :] + got[k, theirs, :]).astype(BF16)


def half_sum_kernel(idx, own, got, t0, t1, t2, t3):
    for k, out in enumerate((t0, t1, t2, t3)):
        out[...] = own[k] + got[k].astype(F32)


def norm_backward_kernel(idx, h, gain, t0, t1, t2, t3, out):
    x, zh, c = idx[0], idx[3], idx[4]
    rows = at(c * 128 + zh * 64, 64, 64)
    h_all = h[rows, :].astype(F32)
    scale = jnp.sqrt(jnp.mean(h_all * h_all, axis=-1, keepdims=True) + epsilon)
    normed, scaled, total = [], [], 0.0
    for k, term in enumerate((t0, t1, t2, t3)):
        columns = at((x + k) % 4 * 512, 512, 512)
        normed.append(h[rows, columns].astype(F32) / scale)
        scaled.append(gain[:, columns] * term[...])
        total = total + jnp.sum(scaled[k] * normed[k], axis=-1, keepdims=True)
    mean = total / 2048
    for k in range(4):
        columns = at((x + k) % 4 * 512, 512, 512)
        out[:, columns] = ((scaled[k] - normed[k] * mean) / scale).astype(BF16)


def y_sum_kernel(idx, own, g1, g2, g3, w, mine, g0, s1, s2, s3):
    zl = idx[2]
    lane = lax.broadcasted_iota(jnp.int32, (32, 128), 1)
    for k, out in enumerate((mine, s1, s2, s3)):
        rows = at((zl + k) % 4 * 32, 32, 32)
        total = own[rows, :] + g1[rows, :].astype(F32) + g2[rows, :].astype(F32) + g3[rows, :].astype(F32)
        back = (4 - k) % 4
        gain_term = jnp.sum(total * w[back * 32 : (back + 1) * 32, :].astype(F32), axis=-1, keepdims=True)
        if k == 0:
            mine[...] = total
            g0[...] = jnp.broadcast_to(gain_term, (32, 128))
        else:
            out[:, :2048] = total.astype(BF16)
            high = gain_term.astype(BF16).astype(F32)
            out[:, 2048:] = jnp.where(lane == 0, high, jnp.where(lane == 1, gain_term - high, 0.0)).astype(BF16)


def z_sum_kernel(idx, mine, g0, s1, s2, s3, out, gain_out):
    out[...] = (mine[...] + s1[:, :2048].astype(F32) + s2[:, :2048].astype(F32) + s3[:, :2048].astype(F32)) * (1.0 / 64)
    tail = s1[:, 2048:].astype(F32) + s2[:, 2048:].astype(F32) + s3[:, 2048:].astype(F32)
    gain_out[...] = g0[...] + jnp.sum(tail, axis=-1, keepdims=True)


def program(hidden, gain, w_value, d_value):
    flat = lax.axis_index("dp") * 4 + lax.axis_index("pipe")
    idx = (flat // jnp.array([64, 4, 16, 2, 1])) % jnp.array([4, 4, 4, 2, 2])
    zh, c = idx[3], idx[4]
    d, w = d_value[0], w_value[0]
    gain_row = gain.reshape(1, 2048)

    d0, d1 = d[:128], d[128:]
    l0 = send(d0, dx=1)
    r1 = send(d1, dx=3)
    w1, w2, w3 = (send(w, dl=k) for k in (1, 2, 3))
    l1 = send(d1, dx=1)
    r0 = send(d0, dx=3)

    e_own, e1, e2, e3 = call(
        norm_kernel, [((256, 512), BF16)] + [((128, 512), BF16)] * 3, 3_000_000, idx, hidden, gain_row,
        scratch=[pltpu.VMEM((256, 128), F32)],
    )
    m1 = send(e1, dx=1)
    m3 = send(e3, dx=3)
    m2 = send(e2, dx=2)
    fa = send(l0, dx=1)
    fb = send(r1, dx=3)
    z_rows = jnp.concatenate([w, w1, w2, w3])
    y1, y3, y2 = (send(z_rows, dy=k) for k in (1, 3, 2))
    oth = send(jnp.stack([m1, m2, m3]), dc=1)

    keep, give = call(
        encoded_grad_kernel, [((4, 128, 512), F32)] * 2, 2_147_000_000,
        idx, z_rows, y1, y2, y3, d0, d1, l0, l1, fa, fb, r0, r1, scratch=[pltpu.VMEM((512, 2048), BF16)],
    )
    got = send(give, dc=1)
    v_own, v1, v2, v3 = call(
        value_kernel, [((128, 2048), F32)] + [((128, 2048), BF16)] * 3, 2_147_000_000,
        idx, e_own, m1, m2, m3, oth, d0, d1, l0, l1, fa, fb, r0, r1, scratch=[pltpu.VMEM((512, 256), F32)],
    )
    own, give = call(core_sum_kernel, [((4, 64, 512), F32), ((4, 64, 512), BF16)], 1_000_000, idx, keep, got)
    got = send(give, dh=1)
    v1, v3, v2 = send(v1, dy=1), send(v3, dy=3), send(v2, dy=2)
    t0, t1, t2, t3 = call(half_sum_kernel, [((64, 512), F32)] * 4, 1_000_000, idx, own, got)
    t1, t3, t2 = send(t1, dx=3), send(t3, dx=1), send(t2, dx=2)
    mine, g0, s1, s2, s3 = call(
        y_sum_kernel, [((32, 2048), F32), ((32, 128), F32)] + [((32, 2176), BF16)] * 3, 1_000_000,
        idx, v_own, v1, v2, v3, z_rows,
    )
    s1, s2, s3 = send(s1, dl=1), send(s2, dl=2), send(s3, dl=3)
    (result,) = call(norm_backward_kernel, [((64, 2048), BF16)], 1_000_000, idx, hidden, gain_row, t0, t1, t2, t3)
    across = send(result, dh=1)
    result_c = send(result, dc=1)
    grad_value, g = call(z_sum_kernel, [((32, 2048), F32), ((32, 128), F32)], 1_000_000, idx, mine, g0, s1, s2, s3)
    g = g + send(g, dc=1)
    across_c = send(across, dc=1)
    g = g + send(g, dh=1)

    same = jnp.where(zh == 0, jnp.stack([result, across]), jnp.stack([across, result]))
    other = jnp.where(zh == 0, jnp.stack([result_c, across_c]), jnp.stack([across_c, result_c]))
    grad_hidden = jnp.where(c == 0, jnp.stack([same, other]), jnp.stack([other, same])).reshape(256, 2048)
    grad_gain = g[:, 0] / (64 * lax.dynamic_slice(gain, (flat // 4 * 32,), (32,)))
    return (grad_hidden, grad_gain, grad_value[None])


def solution(mesh):
    return jax.shard_map(
        program,
        mesh=mesh,
        in_specs=(P("dp", None), P(), P("pipe", "dp", None), P("pipe", "dp", None)),
        out_specs=(P("dp", None), P("dp"), P("pipe", "dp", None)),
        check_vma=False,
    )
```

```python
import functools

import jax
import jax.numpy as jnp
from jax import lax
from jax.experimental import pallas as pl
from jax.experimental.pallas import tpu as pltpu
from jax.sharding import PartitionSpec as P


epsilon = 1e-06
F32, BF16 = jnp.float32, jnp.bfloat16
AXES = ("dp", "pipe")
VMEM = pl.BlockSpec(memory_space=pltpu.VMEM)
SMEM = pl.BlockSpec(memory_space=pltpu.SMEM)


def pairs(dx=0, dy=0, dl=0, dh=0, dc=0):
    out = []
    for x in range(4):
        for zl in range(4):
            for y in range(4):
                for zh in range(2):
                    for c in range(2):
                        source = (((x * 4 + zl) * 4 + y) * 2 + zh) * 2 + c
                        target = ((((x + dx) % 4 * 4 + (zl + dl) % 4) * 4 + (y + dy) % 4) * 2 + (zh + dh) % 2) * 2 + (c + dc) % 2
                        out.append((source, target))
    return out


def send(value, **shift):
    return lax.ppermute(value, AXES, pairs(**shift))


def call(body, outs, flops, *args, scratch=(), mib=8):
    shapes = [jax.ShapeDtypeStruct(s, t) for s, t in outs]
    moved = sum(v.size * v.dtype.itemsize for v in args) + sum(v.size * v.dtype.itemsize for v in shapes)
    return pl.pallas_call(
        body,
        out_shape=shapes,
        in_specs=[SMEM] + [VMEM] * (len(args) - 1),
        out_specs=[VMEM] * len(shapes),
        scratch_shapes=list(scratch),
        cost_estimate=pl.CostEstimate(flops=flops, bytes_accessed=moved, transcendentals=0),
        compiler_params=pltpu.CompilerParams(vmem_limit_bytes=mib * 1024 * 1024),
    )(*args)


def at(start, size, multiple):
    return pl.ds(pl.multiple_of(start, multiple), size)


def norm_kernel(idx, h, gain, own, p1, p2, p3, scale):
    x, c = idx[0], idx[4]
    h_all = h[...].astype(F32)
    scale[...] = jnp.broadcast_to(jnp.sqrt(jnp.mean(h_all * h_all, axis=-1, keepdims=True) + epsilon), (256, 128))
    columns = at(x * 512, 512, 512)
    own[...] = (h[:, columns].astype(F32) / scale[:, :1] * gain[:, columns]).T.astype(BF16)
    rows = at(c * 128, 128, 128)
    for k, out in ((1, p1), (2, p2), (3, p3)):
        columns = at((x + k) % 4 * 512, 512, 512)
        out[...] = (h[rows, columns].astype(F32) / scale[rows, :1] * gain[:, columns]).T.astype(BF16)


def dot(a, b, contract=0):
    return lax.dot_general(a, b, (((1,), (contract,)), ((), ())), preferred_element_type=F32)


def value_near_kernel(idx, e_own, m1, m3, oth, d, l, r, acc, e):
    c = idx[4]
    for k, mine, other in ((0, m1, 0), (1, m3, 2)):
        e[:, at(k * 256 + c * 128, 128, 128)] = mine[...]
        e[:, at(k * 256 + (1 - c) * 128, 128, 128)] = oth[other]

    def column(j, carry):
        columns = at(j * 256, 256, 256)
        acc[:, columns] = dot(e_own[...], d[:, columns]) + dot(e[:, :256], l[:, columns]) + dot(e[:, 256:], r[:, columns])
        return carry

    lax.fori_loop(0, 8, column, 0)


def value_far_kernel(start, idx, m2, oth, acc, fa, fb, own, s1, s2, s3, e, tmp):
    y, c = idx[1], idx[4]
    e[:, at(c * 128, 128, 128)] = m2[...]
    e[:, at((1 - c) * 128, 128, 128)] = oth[1]

    def column(j, carry):
        columns, source = at(j * 256, 256, 256), at(start + j * 256, 256, 256)
        tmp[...] = acc[:, source] + dot(e[:, :128], fa[:, source]) + dot(e[:, 128:], fb[:, source])
        for zl in range(4):
            rows = pl.ds(zl * 32, 32)
            own[rows, columns] = tmp[at(zl * 128 + y * 32, 32, 32), :]
            for k, out in ((1, s1), (2, s2), (3, s3)):
                out[rows, columns] = tmp[at(zl * 128 + (y + k) % 4 * 32, 32, 32), :].astype(BF16)
        return carry

    lax.fori_loop(0, 4, column, 0)


def grad_kernel(idx, w0, w1, w2, w3, d, l, fa, fb, r, keep, give, w):
    y, zl, c = idx[1], idx[2], idx[4]
    for k, block in enumerate((w0, w1, w2, w3)):
        jy = (y + 4 - k) % 4
        for back in range(4):
            jz = (zl + 4 - back) % 4
            w[at((jz * 4 + jy) * 32, 32, 32), :] = block[back * 32 : (back + 1) * 32, :]

    def column(j, carry):
        columns = at(j * 256, 256, 256)
        part = w[columns, :]
        for k, block in enumerate((d, l, None, r)):
            if block is None:
                p_a, p_b = dot(fa[...], part, 1), dot(fb[...], part, 1)
            else:
                p = dot(block[...], part, 1)
                p_a, p_b = p[:128], p[128:]
            keep[k, :, columns] = jnp.where(c == 0, p_a, p_b)
            give[k, :, columns] = jnp.where(c == 0, p_b, p_a)
        return carry

    lax.fori_loop(0, 2, column, 0)


def core_sum_kernel(idx, keep, got, own, give):
    zh = idx[3]
    mine, theirs = at(zh * 64, 64, 64), at((1 - zh) * 64, 64, 64)
    for k in range(keep.shape[0]):
        own[k] = keep[k, mine, :] + got[k, mine, :]
        give[k] = (keep[k, theirs, :] + got[k, theirs, :]).astype(BF16)


def half_sum_kernel(idx, own, got, *outs):
    for k, out in enumerate(outs):
        out[...] = own[k] + got[k].astype(F32)


def norm_backward_kernel(idx, h, gain, t0, t1, t2, t3, g, out):
    x, zh, c = idx[0], idx[3], idx[4]
    rows = at(c * 128 + zh * 64, 64, 64)
    h_all = h[rows, :].astype(F32)
    scale = jnp.sqrt(jnp.mean(h_all * h_all, axis=-1, keepdims=True) + epsilon)
    normed, scaled, total = [], [], 0.0
    for k, term in enumerate((t0, t1, t2, t3)):
        columns = at((x + k) % 4 * 512, 512, 512)
        normed.append(h[rows, columns].astype(F32) / scale)
        scaled.append(gain[:, columns] * term[...])
        total = total + jnp.sum(scaled[k] * normed[k], axis=-1, keepdims=True)
    mean = total / 2048
    for k in range(4):
        columns = at((x + k) % 4 * 512, 512, 512)
        out[:, columns] = ((scaled[k] - normed[k] * mean) / scale).astype(BF16)
    lane = lax.broadcasted_iota(jnp.int32, (32, 128), 1)
    high = g[...].astype(BF16).astype(F32)
    middle = (g[...] - high).astype(BF16).astype(F32)
    low = g[...] - high - middle
    out[:32, 2048:] = jnp.where(lane == 0, high, jnp.where(lane == 1, middle, jnp.where(lane == 2, low, 0.0))).astype(BF16)
    out[32:, 2048:] = jnp.zeros((32, 128), BF16)


def final_kernel(idx, divisor, own, across, own_c, across_c, out, gain_out):
    zh, c = idx[3], idx[4]
    for block, other_h, other_c in ((own, 0, 0), (across, 1, 0), (own_c, 0, 1), (across_c, 1, 1)):
        out[at(((c + other_c) % 2 * 2 + (zh + other_h) % 2) * 64, 64, 64), :] = block[:, :2048]

    def term(block):
        return jnp.sum(block[:32, 2048:].astype(F32), axis=-1, keepdims=True)

    total = (term(own) + term(own_c)) + (term(across) + term(across_c))
    gain_out[...] = jnp.broadcast_to(total, (32, 128)).T[:1, :] / divisor[...]


def y_sum_kernel(start, idx, own, g1, g2, g3, w, mine, g0, s1, s2, s3):
    zl = idx[2]
    lane = lax.broadcasted_iota(jnp.int32, (32, 128), 1)
    for k, out in enumerate((mine, s1, s2, s3)):
        rows = at((zl + k) % 4 * 32, 32, 32)
        total = own[rows, :] + g1[rows, :].astype(F32) + g2[rows, :].astype(F32) + g3[rows, :].astype(F32)
        back = (4 - k) % 4
        w_part = w[back * 32 : (back + 1) * 32, start : start + 1024].astype(F32)
        gain_term = jnp.sum(total * w_part, axis=-1, keepdims=True)
        if k == 0:
            mine[...] = total
            g0[...] = jnp.broadcast_to(gain_term, (32, 128))
        else:
            out[:, :1024] = total.astype(BF16)
            high = gain_term.astype(BF16).astype(F32)
            out[:, 1024:] = jnp.where(lane == 0, high, jnp.where(lane == 1, gain_term - high, 0.0)).astype(BF16)


def z_sum_kernel(idx, mine_a, g_a, a1, a2, a3, mine_b, g_b, b1, b2, b3, out, gain_out):
    total = g_a[...] + g_b[...]
    for start, mine, s1, s2, s3 in ((0, mine_a, a1, a2, a3), (1024, mine_b, b1, b2, b3)):
        part = mine[...] + s1[:, :1024].astype(F32) + s2[:, :1024].astype(F32) + s3[:, :1024].astype(F32)
        out[:, start : start + 1024] = part * (1.0 / 64)
        tail = s1[:, 1024:].astype(F32) + s2[:, 1024:].astype(F32) + s3[:, 1024:].astype(F32)
        total = total + jnp.sum(tail, axis=-1, keepdims=True)
    gain_out[...] = total


def program(hidden, gain, w_value, d_value):
    flat = lax.axis_index("dp") * 4 + lax.axis_index("pipe")
    idx = (flat // jnp.array([64, 4, 16, 2, 1])) % jnp.array([4, 4, 4, 2, 2])
    d, w = d_value[0], w_value[0]
    gain_row = gain.reshape(1, 2048)

    l, r = send(d, dx=1), send(d, dx=3)
    w1, w3, w2 = (send(w, dl=k) for k in (1, 3, 2))
    e_own, e1, e2, e3 = call(
        norm_kernel, [((512, 256), BF16)] + [((512, 128), BF16)] * 3, 3_000_000, idx, hidden, gain_row,
        scratch=[pltpu.VMEM((256, 128), F32)],
    )
    m1, m3, m2 = send(e1, dx=1), send(e3, dx=3), send(e2, dx=2)
    z_rows = jnp.concatenate([w, w1, w2, w3])
    y1, y3, y2 = (send(z_rows, dy=k) for k in (1, 3, 2))
    oth = send(jnp.stack([m1, m2, m3]), dc=1)
    l_half, r_half = l[:128], r[128:]
    fa, fb = send(l_half, dx=1), send(r_half, dx=3)

    (acc,) = call(
        value_near_kernel, [((512, 2048), F32)], 1_610_000_000, idx, e_own, m1, m3, oth, d, l, r,
        scratch=[pltpu.VMEM((512, 512), BF16)], mib=20,
    )
    keep, give = call(
        grad_kernel, [((4, 128, 512), F32)] * 2, 2_147_000_000, idx, z_rows, y1, y2, y3, d, l, fa, fb, r,
        scratch=[pltpu.VMEM((512, 2048), BF16)], mib=20,
    )
    got = send(give, dc=1)

    def far(start):
        return call(
            functools.partial(value_far_kernel, start), [((128, 1024), F32)] + [((128, 1024), BF16)] * 3,
            268_000_000, idx, m2, oth, acc, fa, fb,
            scratch=[pltpu.VMEM((512, 256), BF16), pltpu.VMEM((512, 256), F32)], mib=20,
        )

    def y_sum(start, v_own, v1, v2, v3):
        v1, v3, v2 = send(v1, dy=1), send(v3, dy=3), send(v2, dy=2)
        mine, g0, s1, s2, s3 = call(
            functools.partial(y_sum_kernel, start),
            [((32, 1024), F32), ((32, 128), F32)] + [((32, 1152), BF16)] * 3, 1_000_000, idx, v_own, v1, v2, v3, z_rows,
        )
        return mine, g0, send(s1, dl=1), send(s2, dl=2), send(s3, dl=3)

    parts = []
    for start in (0, 1024):
        parts.extend(y_sum(start, *far(start)))

    own, give = call(core_sum_kernel, [((4, 64, 512), F32), ((4, 64, 512), BF16)], 1_000_000, idx, keep, got)
    got = send(give, dh=1)
    t0, t1, t2, t3 = call(half_sum_kernel, [((64, 512), F32)] * 4, 1_000_000, idx, own, got)
    t1, t3, t2 = send(t1, dx=3), send(t3, dx=1), send(t2, dx=2)
    grad_value, g = call(z_sum_kernel, [((32, 2048), F32), ((32, 128), F32)], 1_000_000, idx, *parts)
    (result,) = call(norm_backward_kernel, [((64, 2176), BF16)], 1_000_000, idx, hidden, gain_row, t0, t1, t2, t3, g)
    across, result_c = send(result, dh=1), send(result, dc=1)
    across_c = send(across, dc=1)
    divisor = 64 * lax.dynamic_slice(gain_row, (0, flat // 4 * 32), (1, 32))
    grad_hidden, g = call(
        final_kernel, [((256, 2048), BF16), ((1, 32), F32)], 1_000_000,
        idx, divisor, result, across, result_c, across_c,
    )
    grad_gain = g.reshape(32)
    return (grad_hidden, grad_gain, grad_value[None])


def solution(mesh):
    return jax.shard_map(
        program,
        mesh=mesh,
        in_specs=(P("dp", None), P(), P("pipe", "dp", None), P("pipe", "dp", None)),
        out_specs=(P("dp", None), P("dp"), P("pipe", "dp", None)),
        check_vma=False,
    )
```

```python
import functools

import jax
import jax.numpy as jnp
from jax import lax
from jax.experimental import pallas as pl
from jax.experimental.pallas import tpu as pltpu
from jax.sharding import PartitionSpec as P


epsilon = 1e-06
F32, BF16 = jnp.float32, jnp.bfloat16
AXES = ("dp", "pipe")
VMEM = pl.BlockSpec(memory_space=pltpu.VMEM)
SMEM = pl.BlockSpec(memory_space=pltpu.SMEM)


def pairs(dx=0, dy=0, dl=0, dh=0, dc=0):
    out = []
    for x in range(4):
        for zl in range(4):
            for y in range(4):
                for zh in range(2):
                    for c in range(2):
                        source = (((x * 4 + zl) * 4 + y) * 2 + zh) * 2 + c
                        target = ((((x + dx) % 4 * 4 + (zl + dl) % 4) * 4 + (y + dy) % 4) * 2 + (zh + dh) % 2) * 2 + (c + dc) % 2
                        out.append((source, target))
    return out


def send(value, **shift):
    return lax.ppermute(value, AXES, pairs(**shift))


def call(body, outs, flops, *args, scratch=(), mib=8):
    shapes = [jax.ShapeDtypeStruct(s, t) for s, t in outs]
    moved = sum(v.size * v.dtype.itemsize for v in args) + sum(v.size * v.dtype.itemsize for v in shapes)
    return pl.pallas_call(
        body,
        out_shape=shapes,
        in_specs=[SMEM] + [VMEM] * (len(args) - 1),
        out_specs=[VMEM] * len(shapes),
        scratch_shapes=list(scratch),
        cost_estimate=pl.CostEstimate(flops=flops, bytes_accessed=moved, transcendentals=0),
        compiler_params=pltpu.CompilerParams(vmem_limit_bytes=mib * 1024 * 1024),
    )(*args)


def at(start, size, multiple):
    return pl.ds(pl.multiple_of(start, multiple), size)


def norm_kernel(idx, h, gain, own, p1, p2, p3, scale):
    x, c = idx[0], idx[4]
    h_all = h[...].astype(F32)
    scale[...] = jnp.broadcast_to(jnp.sqrt(jnp.mean(h_all * h_all, axis=-1, keepdims=True) + epsilon), (256, 128))
    columns = at(x * 512, 512, 512)
    own[...] = (h[:, columns].astype(F32) / scale[:, :1] * gain[:, columns]).T.astype(BF16)
    rows = at(c * 128, 128, 128)
    for k, out in ((1, p1), (2, p2), (3, p3)):
        columns = at((x + k) % 4 * 512, 512, 512)
        out[...] = (h[rows, columns].astype(F32) / scale[rows, :1] * gain[:, columns]).T.astype(BF16)


def dot(a, b, contract=0):
    return lax.dot_general(a, b, (((1,), (contract,)), ((), ())), preferred_element_type=F32)


def value_near_kernel(idx, e_own, m1, m3, oth, d, l, r, acc, e):
    c = idx[4]
    for k, mine, other in ((0, m1, 0), (1, m3, 2)):
        e[:, at(k * 256 + c * 128, 128, 128)] = mine[...]
        e[:, at(k * 256 + (1 - c) * 128, 128, 128)] = oth[other]

    def column(j, carry):
        columns = at(j * 256, 256, 256)
        acc[:, columns] = dot(e_own[...], d[:, columns]) + dot(e[:, :256], l[:, columns]) + dot(e[:, 256:], r[:, columns])
        return carry

    lax.fori_loop(0, 8, column, 0)


def value_far_kernel(start, idx, m2, oth, acc, fa, fb, own, s1, s2, s3, e, tmp):
    y, c = idx[1], idx[4]
    e[:, at(c * 128, 128, 128)] = m2[...]
    e[:, at((1 - c) * 128, 128, 128)] = oth[1]

    def column(j, carry):
        columns, source = at(j * 256, 256, 256), at(start + j * 256, 256, 256)
        tmp[...] = acc[:, source] + dot(e[:, :128], fa[:, columns]) + dot(e[:, 128:], fb[:, columns])
        for zl in range(4):
            rows = pl.ds(zl * 32, 32)
            own[rows, columns] = tmp[at(zl * 128 + y * 32, 32, 32), :]
            for k, out in ((1, s1), (2, s2), (3, s3)):
                out[rows, columns] = tmp[at(zl * 128 + (y + k) % 4 * 32, 32, 32), :].astype(BF16)
        return carry

    lax.fori_loop(0, 4, column, 0)


def grad_kernel(idx, w0, w1, w2, w3, d, l, fa0, fb0, fa1, fb1, r, keep, give, w):
    y, zl, c = idx[1], idx[2], idx[4]
    for k, block in enumerate((w0, w1, w2, w3)):
        jy = (y + 4 - k) % 4
        for back in range(4):
            jz = (zl + 4 - back) % 4
            w[at((jz * 4 + jy) * 32, 32, 32), :] = block[back * 32 : (back + 1) * 32, :]

    def column(j, carry):
        columns = at(j * 256, 256, 256)
        part = w[columns, :]
        for k, block in enumerate((d, l, None, r)):
            if block is None:
                p_a = dot(fa0[...], part[:, :1024], 1) + dot(fa1[...], part[:, 1024:], 1)
                p_b = dot(fb0[...], part[:, :1024], 1) + dot(fb1[...], part[:, 1024:], 1)
            else:
                p = dot(block[...], part, 1)
                p_a, p_b = p[:128], p[128:]
            keep[k, :, columns] = jnp.where(c == 0, p_a, p_b)
            give[k, :, columns] = jnp.where(c == 0, p_b, p_a)
        return carry

    lax.fori_loop(0, 2, column, 0)


def core_sum_kernel(idx, keep, got, own, give):
    zh = idx[3]
    mine, theirs = at(zh * 64, 64, 64), at((1 - zh) * 64, 64, 64)
    for k in range(keep.shape[0]):
        own[k] = keep[k, mine, :] + got[k, mine, :]
        give[k] = (keep[k, theirs, :] + got[k, theirs, :]).astype(BF16)


def half_sum_kernel(idx, own, got, *outs):
    for k, out in enumerate(outs):
        out[...] = own[k] + got[k].astype(F32)


def norm_backward_kernel(idx, h, gain, t0, t1, t2, t3, g, out):
    x, zh, c = idx[0], idx[3], idx[4]
    rows = at(c * 128 + zh * 64, 64, 64)
    h_all = h[rows, :].astype(F32)
    scale = jnp.sqrt(jnp.mean(h_all * h_all, axis=-1, keepdims=True) + epsilon)
    normed, scaled, total = [], [], 0.0
    for k, term in enumerate((t0, t1, t2, t3)):
        columns = at((x + k) % 4 * 512, 512, 512)
        normed.append(h[rows, columns].astype(F32) / scale)
        scaled.append(gain[:, columns] * term[...])
        total = total + jnp.sum(scaled[k] * normed[k], axis=-1, keepdims=True)
    mean = total / 2048
    for k in range(4):
        columns = at((x + k) % 4 * 512, 512, 512)
        out[:, columns] = ((scaled[k] - normed[k] * mean) / scale).astype(BF16)
    lane = lax.broadcasted_iota(jnp.int32, (32, 128), 1)
    high = g[...].astype(BF16).astype(F32)
    middle = (g[...] - high).astype(BF16).astype(F32)
    low = g[...] - high - middle
    out[:32, 2048:] = jnp.where(lane == 0, high, jnp.where(lane == 1, middle, jnp.where(lane == 2, low, 0.0))).astype(BF16)
    out[32:, 2048:] = jnp.zeros((32, 128), BF16)


def final_kernel(idx, divisor, own, across, own_c, across_c, out, gain_out):
    zh, c = idx[3], idx[4]
    for block, other_h, other_c in ((own, 0, 0), (across, 1, 0), (own_c, 0, 1), (across_c, 1, 1)):
        out[at(((c + other_c) % 2 * 2 + (zh + other_h) % 2) * 64, 64, 64), :] = block[:, :2048]

    def term(block):
        return jnp.sum(block[:32, 2048:].astype(F32), axis=-1, keepdims=True)

    total = (term(own) + term(own_c)) + (term(across) + term(across_c))
    gain_out[...] = jnp.broadcast_to(total, (32, 128)).T[:1, :] / divisor[...]


def y_sum_kernel(start, idx, own, g1, g2, g3, w, mine, g0, s1, s2, s3):
    zl = idx[2]
    lane = lax.broadcasted_iota(jnp.int32, (32, 128), 1)
    for k, out in enumerate((mine, s1, s2, s3)):
        rows = at((zl + k) % 4 * 32, 32, 32)
        total = own[rows, :] + g1[rows, :].astype(F32) + g2[rows, :].astype(F32) + g3[rows, :].astype(F32)
        back = (4 - k) % 4
        w_part = w[back * 32 : (back + 1) * 32, start : start + 1024].astype(F32)
        gain_term = jnp.sum(total * w_part, axis=-1, keepdims=True)
        if k == 0:
            mine[...] = total
            g0[...] = jnp.broadcast_to(gain_term, (32, 128))
        else:
            out[:, :1024] = total.astype(BF16)
            high = gain_term.astype(BF16).astype(F32)
            out[:, 1024:] = jnp.where(lane == 0, high, jnp.where(lane == 1, gain_term - high, 0.0)).astype(BF16)


def z_sum_kernel(idx, mine_a, g_a, a1, a2, a3, mine_b, g_b, b1, b2, b3, out, gain_out):
    total = g_a[...] + g_b[...]
    for start, mine, s1, s2, s3 in ((0, mine_a, a1, a2, a3), (1024, mine_b, b1, b2, b3)):
        part = mine[...] + s1[:, :1024].astype(F32) + s2[:, :1024].astype(F32) + s3[:, :1024].astype(F32)
        out[:, start : start + 1024] = part * (1.0 / 64)
        tail = s1[:, 1024:].astype(F32) + s2[:, 1024:].astype(F32) + s3[:, 1024:].astype(F32)
        total = total + jnp.sum(tail, axis=-1, keepdims=True)
    gain_out[...] = total


def program(hidden, gain, w_value, d_value):
    flat = lax.axis_index("dp") * 4 + lax.axis_index("pipe")
    idx = (flat // jnp.array([64, 4, 16, 2, 1])) % jnp.array([4, 4, 4, 2, 2])
    d, w = d_value[0], w_value[0]
    gain_row = gain.reshape(1, 2048)

    l, r = send(d, dx=1), send(d, dx=3)
    w1, w3, w2 = (send(w, dl=k) for k in (1, 3, 2))
    e_own, e1, e2, e3 = call(
        norm_kernel, [((512, 256), BF16)] + [((512, 128), BF16)] * 3, 3_000_000, idx, hidden, gain_row,
        scratch=[pltpu.VMEM((256, 128), F32)],
    )
    m1, m3, m2 = send(e1, dx=1), send(e3, dx=3), send(e2, dx=2)
    z_rows = jnp.concatenate([w, w1, w2, w3])
    y1, y3, y2 = (send(z_rows, dy=k) for k in (1, 3, 2))
    oth = send(jnp.stack([m1, m2, m3]), dc=1)
    l_halves = [l[:128, at : at + 1024] for at in (0, 1024)]
    r_halves = [r[128:, at : at + 1024] for at in (0, 1024)]
    fa0, fb0 = send(l_halves[0], dx=1), send(r_halves[0], dx=3)
    fa1, fb1 = send(l_halves[1], dx=1), send(r_halves[1], dx=3)

    (acc,) = call(
        value_near_kernel, [((512, 2048), F32)], 1_610_000_000, idx, e_own, m1, m3, oth, d, l, r,
        scratch=[pltpu.VMEM((512, 512), BF16)], mib=20,
    )
    keep, give = call(
        grad_kernel, [((4, 128, 512), F32)] * 2, 2_147_000_000, idx, z_rows, y1, y2, y3, d, l, fa0, fb0, fa1, fb1, r,
        scratch=[pltpu.VMEM((512, 2048), BF16)], mib=20,
    )
    got = send(give, dc=1)

    def far(start):
        return call(
            functools.partial(value_far_kernel, start), [((128, 1024), F32)] + [((128, 1024), BF16)] * 3,
            268_000_000, idx, m2, oth, acc, *((fa0, fb0) if start == 0 else (fa1, fb1)),
            scratch=[pltpu.VMEM((512, 256), BF16), pltpu.VMEM((512, 256), F32)], mib=20,
        )

    def y_sum(start, v_own, v1, v2, v3):
        v1, v3, v2 = send(v1, dy=1), send(v3, dy=3), send(v2, dy=2)
        mine, g0, s1, s2, s3 = call(
            functools.partial(y_sum_kernel, start),
            [((32, 1024), F32), ((32, 128), F32)] + [((32, 1152), BF16)] * 3, 1_000_000, idx, v_own, v1, v2, v3, z_rows,
        )
        return mine, g0, send(s1, dl=1), send(s2, dl=2), send(s3, dl=3)

    parts = []
    for start in (0, 1024):
        parts.extend(y_sum(start, *far(start)))

    own, give = call(core_sum_kernel, [((4, 64, 512), F32), ((4, 64, 512), BF16)], 1_000_000, idx, keep, got)
    got = send(give, dh=1)
    t0, t1, t2, t3 = call(half_sum_kernel, [((64, 512), F32)] * 4, 1_000_000, idx, own, got)
    t1, t3, t2 = send(t1, dx=3), send(t3, dx=1), send(t2, dx=2)
    grad_value, g = call(z_sum_kernel, [((32, 2048), F32), ((32, 128), F32)], 1_000_000, idx, *parts)
    (result,) = call(norm_backward_kernel, [((64, 2176), BF16)], 1_000_000, idx, hidden, gain_row, t0, t1, t2, t3, g)
    across, result_c = send(result, dh=1), send(result, dc=1)
    across_c = send(across, dc=1)
    divisor = 64 * lax.dynamic_slice(gain_row, (0, flat // 4 * 32), (1, 32))
    grad_hidden, g = call(
        final_kernel, [((256, 2048), BF16), ((1, 32), F32)], 1_000_000,
        idx, divisor, result, across, result_c, across_c,
    )
    grad_gain = g.reshape(32)
    return (grad_hidden, grad_gain, grad_value[None])


def solution(mesh):
    return jax.shard_map(
        program,
        mesh=mesh,
        in_specs=(P("dp", None), P(), P("pipe", "dp", None), P("pipe", "dp", None)),
        out_specs=(P("dp", None), P("dp"), P("pipe", "dp", None)),
        check_vma=False,
    )
```
